32 devices in a mesh: layer: 4 (over y, x), strip: 8 (over z, core).
Axes of the slice: x: 2, y: 2, z: 4, core: 2. Of those that a mesh axis runs over, the one named last changes fastest.
Arguments:
- launch: bfloat16 [2, 2, 1024, 1024], P(None, None, 'strip'), may hold values from -6 to 6
- screens: float32 [4, 1024, 1024], P('layer', 'strip'), may hold values from -3.140625 to 3.140625
- distance: float32 [4], P('layer'), may hold values from 1024 to 2048
- templates: bfloat16 [1024, 16], replicated, may hold values from -0.1875 to 0.1875
- send_table: int32 [8, 8, 4], P('strip', None, 'layer'), may hold values from 0 to 511, as said below
- send_counts: int32 [8, 8], P('strip'), may hold values from 0 to 4, as said below
Outputs:
- pupil: bfloat16 [2, 2, 1024, 1024], P(None, None, 'strip')
- correlation: float32 [8, 8, 4, 2, 16], P('strip', None, 'layer')
The draws below stay inside these ranges and needn't reach their ends.
Inputs may be any that keep to these rules, and one draw needn't show every extreme that they name: For each source strip s the 8 x 4 entries send_table[s] are distinct subaperture numbers local to that strip (row by row over its 512 subapertures). `send_counts`: some owner receives 4 live slots from every source.
All inputs are finite; a program needn't handle non-finite values.
Results may differ from the reference program's by a relative error of at most 0.03.
Values may be sent and summed in bfloat16 or wider, within the bound.
A program may use at most 64 MiB of HBM per device.

```python
import math
import jax
import jax.numpy as jnp
from jax import lax

N = 1024
SUB = 16
CHANNELS = 16
FIELDS = 2
CAP = 4
LAYERS = 4
SIDE = 64
SUBS_DEV = 512
PIX = 1024
N_STRIP = 8


def routing_tables(key):
    base = jax.random.fold_in(key, 4177)
    order_key, count_key, owner_key = jax.random.split(base, 3)

    def shuffled(single_key):
        return jax.random.permutation(single_key, SUBS_DEV)
    orders = jax.vmap(shuffled)(jax.random.split(order_key, N_STRIP))
    table = orders[:, :N_STRIP * CAP].reshape(N_STRIP, N_STRIP, CAP).astype(jnp.int32)
    counts = jax.random.randint(count_key, (N_STRIP, N_STRIP), 0, CAP + 1, dtype=jnp.int32)
    busiest = jax.random.randint(owner_key, (), 0, N_STRIP, dtype=jnp.int32)
    counts = jnp.where(jnp.arange(N_STRIP, dtype=jnp.int32)[None, :] == busiest, CAP, counts)
    return (table, counts.astype(jnp.int32))


def draw_send_table(key, part):
    return routing_tables(key)[0]


def draw_send_counts(key, part):
    return routing_tables(key)[1]


def levels(rng, extent, shards, smallest, largest):
    def one(dim, parts):
        draws = jax.random.uniform(jax.random.fold_in(jax.random.fold_in(rng, 6), dim), (parts,), jnp.float32, smallest / len(shards), largest / len(shards))
        return jnp.repeat(jnp.exp(draws), extent[dim] // parts).reshape((-1,) + (1,) * (len(extent) - dim - 1))

    level = one(*shards[0])
    for cut in shards[1:]:
        level = level * one(*cut)
    return level


def bell_draw(rng, shape, spread, reach, shards=(), kind=jnp.bfloat16):
    loudness = levels(rng, shape, shards, -0.22, 0.18) if shards else 1.0
    entries = jax.random.normal(rng, shape, jnp.float32) * spread * loudness
    return jnp.minimum(jnp.maximum(entries, -reach), reach).astype(kind)


def setup_inputs(seed: int = 0) -> dict:
    arg_keys = jax.random.split(jax.random.key(seed), 7)
    return {
        "launch": bell_draw(arg_keys[0], (FIELDS, 2, N, N), 1.0, 6.0, ((2, 8),)),
        "screens": jnp.clip(jax.random.uniform(arg_keys[1], (LAYERS, N, N), jnp.float32, -3.140625, 3.140625), -3.140625, 3.140625),
        "distance": jnp.clip(jnp.exp(math.log(2048.0) - 0.6931472 * jax.random.uniform(arg_keys[2], (LAYERS,), jnp.float32) ** levels(arg_keys[2], (LAYERS,), ((0, 4),), -0.2, 0.2)), 1024.0, 2048.0),
        "templates": bell_draw(arg_keys[3], (PIX, CHANNELS), PIX ** -0.5, 0.1875),
        "send_table": draw_send_table(jax.random.fold_in(arg_keys[6], 71), 0),
        "send_counts": draw_send_counts(jax.random.fold_in(arg_keys[6], 71), 0),
    }


def fourier_tables(length):
    counter = jnp.arange(length, dtype=jnp.int32)
    product = counter[:, None] * counter[None, :] % length
    angles = product.astype(jnp.float32) * (2.0 * math.pi / length)
    factor = 1.0 / math.sqrt(length)
    return ((jnp.cos(angles) * factor).astype(jnp.bfloat16), (jnp.sin(angles) * factor).astype(jnp.bfloat16))

def spectral_factor(distance_value, length):
    counter = jnp.arange(length, dtype=jnp.int32)
    signed = jnp.where(counter < length // 2, counter, counter - length).astype(jnp.float32)
    phases = -distance_value * math.pi * signed * signed / float(length * length)
    return (jnp.cos(phases), jnp.sin(phases))

def spot_table(subsize):
    spotsize = 2 * subsize
    outer = jnp.arange(spotsize, dtype=jnp.int32)
    inner = jnp.arange(subsize, dtype=jnp.int32)
    angles = (inner[:, None] * outer[None, :] % spotsize).astype(jnp.float32) * (2.0 * math.pi / spotsize)
    wave_re = jnp.cos(angles) / math.sqrt(subsize)
    wave_im = -jnp.sin(angles) / math.sqrt(subsize)
    kron_re = wave_re[:, None, :, None] * wave_re[None, :, None, :] - wave_im[:, None, :, None] * wave_im[None, :, None, :]
    kron_im = wave_re[:, None, :, None] * wave_im[None, :, None, :] + wave_im[:, None, :, None] * wave_re[None, :, None, :]
    kron_re = kron_re.reshape(subsize * subsize, spotsize * spotsize)
    kron_im = kron_im.reshape(subsize * subsize, spotsize * spotsize)
    upper = jnp.concatenate([kron_re, kron_im], axis=1)
    lower = jnp.concatenate([-kron_im, kron_re], axis=1)
    return jnp.concatenate([upper, lower], axis=0).astype(jnp.bfloat16)

def rounded(value):
    return lax.optimization_barrier(value.astype(jnp.bfloat16)).astype(jnp.float32)

def layer_pass(field, screen, distance_value, cosine_table, sine_table):
    real_part = field[0].astype(jnp.float32)
    imag_part = field[1].astype(jnp.float32)
    screen_cos = jnp.cos(screen)
    screen_sin = jnp.sin(screen)
    screened = rounded(jnp.stack([real_part * screen_cos - imag_part * screen_sin, real_part * screen_sin + imag_part * screen_cos]))
    factor_re, factor_im = spectral_factor(distance_value, field.shape[2])
    along_cos = jnp.einsum('prj,jk->prk', screened, cosine_table)
    along_sin = jnp.einsum('prj,jk->prk', screened, sine_table)
    freq_re = along_cos[0] + along_sin[1]
    freq_im = along_cos[1] - along_sin[0]
    spectrum = rounded(jnp.stack([freq_re * factor_re[None, :] - freq_im * factor_im[None, :], freq_re * factor_im[None, :] + freq_im * factor_re[None, :]]))
    row_cos = jnp.einsum('pjc,jk->pkc', spectrum, cosine_table)
    row_sin = jnp.einsum('pjc,jk->pkc', spectrum, sine_table)
    wave_re = row_cos[0] + row_sin[1]
    wave_im = row_cos[1] - row_sin[0]
    phased = rounded(jnp.stack([wave_re * factor_re[:, None] - wave_im * factor_im[:, None], wave_re * factor_im[:, None] + wave_im * factor_re[:, None]]))
    back_cos = jnp.einsum('pjc,jk->pkc', phased, cosine_table)
    back_sin = jnp.einsum('pjc,jk->pkc', phased, sine_table)
    returned = rounded(jnp.stack([back_cos[0] - back_sin[1], back_cos[1] + back_sin[0]]))
    final_cos = jnp.einsum('prk,kj->prj', returned, cosine_table)
    final_sin = jnp.einsum('prk,kj->prj', returned, sine_table)
    return jnp.stack([final_cos[0] - final_sin[1], final_cos[1] + final_sin[0]]).astype(jnp.bfloat16)

def correlate_slots(slots, big_table, templates):
    pixels = templates.shape[0]
    fields_count = slots.shape[-1] // big_table.shape[0]
    shaped = slots.reshape(slots.shape[:-1] + (fields_count, big_table.shape[0])).astype(jnp.float32)
    spot_field = jnp.einsum('...i,io->...o', shaped, big_table.astype(jnp.float32))
    intensity = spot_field[..., :pixels] * spot_field[..., :pixels] + spot_field[..., pixels:] * spot_field[..., pixels:]
    intensity = rounded(intensity)
    return jnp.einsum('...i,io->...o', intensity, templates.astype(jnp.float32))

def reference(launch, screens, distance, templates, send_table, send_counts):
    cosine_bf, sine_bf = fourier_tables(N)
    cosine_table = cosine_bf.astype(jnp.float32)
    sine_table = sine_bf.astype(jnp.float32)
    finished = []
    for field_index in range(FIELDS):
        current = launch[field_index]
        for layer_index in range(LAYERS):
            current = layer_pass(current, screens[layer_index], distance[layer_index], cosine_table, sine_table)
        finished.append(current)
    pupil = jnp.stack(finished)
    blocks = pupil.reshape(FIELDS, 2, SIDE, SUB, SIDE, SUB).transpose(2, 4, 0, 1, 3, 5)
    blocks = blocks.reshape(SIDE * SIDE, FIELDS * 2 * SUB * SUB)
    offsets = (jnp.arange(N_STRIP, dtype=jnp.int32) * SUBS_DEV)[:, None, None]
    chosen = (send_table + offsets).astype(jnp.int32).reshape(-1)
    gathered = blocks[chosen].reshape(N_STRIP, N_STRIP, CAP, FIELDS * 2 * SUB * SUB)
    live = jnp.arange(CAP, dtype=jnp.int32)[None, None, :] < send_counts[:, :, None]
    gathered = jnp.where(live[:, :, :, None], gathered, jnp.zeros((), jnp.bfloat16))
    big_table = spot_table(SUB)
    correlation = correlate_slots(gathered, big_table, templates)
    return (pupil, correlation.transpose(1, 0, 2, 3, 4))
```

```python
import functools
import math

import jax
import jax.numpy as jnp
import numpy as np
from jax import lax
from jax.experimental import pallas as pl
from jax.experimental.pallas import tpu as pltpu
from jax.sharding import PartitionSpec as P

SUB = 16
F32 = jnp.float32
BF16 = jnp.bfloat16
MESH = pl.DeviceIdType.MESH


def cosine_half_table(length):
    k = np.arange(length // 2, dtype=np.int64)
    n = np.arange(length, dtype=np.int64)
    p = (k[:, None] * n[None, :]) % length
    p = np.minimum(p, length - p)
    return np.cos(2.0 * np.pi * p / length).astype(np.float32).astype(BF16)


def spot_table(subsize):
    spotsize = 2 * subsize
    outer = np.arange(spotsize)
    inner = np.arange(subsize)
    angles = (inner[:, None] * outer[None, :] % spotsize) * (2.0 * np.pi / spotsize)
    wave = (np.cos(angles) - 1j * np.sin(angles)) / math.sqrt(subsize)
    kron = wave[:, None, :, None] * wave[None, :, None, :]
    kron = kron.reshape(subsize * subsize, spotsize * spotsize)
    upper = np.concatenate([kron.real, kron.imag], axis=1)
    lower = np.concatenate([-kron.imag, kron.real], axis=1)
    return np.concatenate([upper, lower], axis=0).astype(np.float32).astype(BF16)


def kernel_line(distance_value, length):
    half = length // 2
    counter = jnp.arange(half + 1, dtype=jnp.int32).astype(F32)
    phases = -distance_value * math.pi * counter * counter / float(length * length)
    h = jnp.stack([jnp.cos(phases), jnp.sin(phases)])
    weight = jnp.where(counter == 0.0, 1.0, 2.0) / length
    folded = (h * weight)[:, :half]
    high = folded.astype(BF16)
    low = (folded - high.astype(F32)).astype(BF16)
    table = jnp.asarray(cosine_half_table(length))
    parts = jnp.dot(jnp.concatenate([high, low]), table, preferred_element_type=F32)
    sign = (1 - 2 * (jnp.arange(length, dtype=jnp.int32) % 2)).astype(F32) / length
    line = parts[:2] + parts[2:] + h[:, half:] * sign
    return jnp.concatenate([line, jnp.zeros((6, length), F32)])


def sincos(x):
    y = 0.5 * x
    z = y * y
    s = -1.0 / 39916800.0
    for c in (1.0 / 362880.0, -1.0 / 5040.0, 1.0 / 120.0, -1.0 / 6.0, 1.0):
        s = s * z + c
    s = s * y
    c0 = 1.0 / 479001600.0
    for c in (-1.0 / 3628800.0, 1.0 / 40320.0, -1.0 / 720.0, 1.0 / 24.0, -0.5, 1.0):
        c0 = c0 * z + c
    return 2.0 * s * c0, 1.0 - 2.0 * s * s


def propagate_kernel(
    layers, strips, launch_ref, scr_ref, scrt_ref, g_ref, out_ref,
    gall, gmat, srow, scol, sendbuf, recvbuf, slab, swapped, mid,
    gsend, grecv, ssend, srecv, xsend, xrecv, osend, orecv,
):
    count = layers * strips
    length = launch_ref.shape[-1]
    lines = launch_ref.shape[-2]
    wide = 4 * lines
    sec = lax.axis_index("layer")
    strip = lax.axis_index("strip")
    me = strip * layers + sec

    barrier = pltpu.get_barrier_semaphore()

    def greet(k, _):
        peer = lax.rem(me + k, count)
        pl.semaphore_signal(
            barrier, inc=1, device_id=(lax.rem(peer, layers), peer // layers), device_id_type=MESH
        )
        return 0

    lax.fori_loop(1, count, greet, 0)
    pl.semaphore_wait(barrier, count - 1)

    def remote(src, dst, ssem, rsem, a, s):
        return pltpu.make_async_remote_copy(
            src_ref=src, dst_ref=dst, send_sem=ssem, recv_sem=rsem,
            device_id=(a, s), device_id_type=MESH,
        )

    for k in range(1, layers):
        a = lax.rem(sec + k, layers)
        remote(g_ref, gall.at[sec], gsend, grecv.at[sec], a, strip).start()
    for lay in range(layers):
        if lay % 2 == 0:
            @pl.when(sec == lay)
            def _(lay=lay):
                for k in range(1, layers):
                    a = lax.rem(sec + k, layers)
                    remote(scr_ref.at[a], srow.at[lay // 2], ssend, srecv.at[lay], a, strip).start()
                srow[lay // 2] = scr_ref[lay]
        else:
            @pl.when(sec == lay)
            def _(lay=lay):
                def give(k, _):
                    peer = lax.rem(me + k, count)
                    remote(
                        scrt_ref.at[peer], scol.at[lay // 2, strip], ssend, srecv.at[lay],
                        lax.rem(peer, layers), peer // layers,
                    ).start()
                    return 0

                lax.fori_loop(1, count, give, 0)
                scol[lay // 2, strip] = scrt_ref[me]
    gall[sec] = g_ref[...]

    def build(lay):
        @pl.when(sec != lay)
        def _():
            remote(g_ref, gall.at[lay], gsend, grecv.at[lay], sec, strip).wait_recv()

        band = 128
        for part in range(2):
            row = gall[lay, part:part + 1, :]
            base = pltpu.roll(
                jnp.broadcast_to(row, (band, length)), 0, axis=1, stride=1, stride_axis=0
            ).astype(BF16)
            for b in range(length // band):
                at = band * b
                if b:
                    gmat[lay, part, at:at + band, 0:at] = base[:, length - at:]
                gmat[lay, part, at:at + band, at:] = base[:, :length - at]

    def screen_of(lay):
        if lay % 2 == 0:
            @pl.when(sec != lay)
            def _():
                remote(scr_ref.at[0], srow.at[lay // 2], ssend, srecv.at[lay], sec, strip).wait_recv()
            return sincos(srow[lay // 2])

        @pl.when(sec != lay)
        def _():
            whole = scol.at[lay // 2]
            remote(whole, whole, ssend, srecv.at[lay], sec, strip).wait_recv()

        @pl.when(sec == lay)
        def _():
            most = scol.at[lay // 2, pl.ds(0, strips - 1)]
            remote(most, most, ssend, srecv.at[lay], sec, strip).wait_recv()

        theta = jnp.concatenate([scol[lay // 2, s] for s in range(strips)], axis=1)
        return sincos(theta)

    def put(fc, value):
        rounded = value.astype(BF16)
        slab[fc * lines:(fc + 1) * lines, :] = rounded
        other = fc ^ 1
        swapped[other * lines:(other + 1) * lines, :] = rounded if fc % 2 == 0 else -rounded

    def screened(lay, load):
        sine, cosine = screen_of(lay)
        for f in range(2):
            re = load(2 * f)
            im = load(2 * f + 1)
            put(2 * f, re * cosine - im * sine)
            put(2 * f + 1, re * sine + im * cosine)

    block = 256

    def across(lay, step):
        def body(b, _):
            at = pl.ds(pl.multiple_of(b * block, block), block)
            dims = (((1,), (1,)), ((), ()))
            total = lax.dot_general(
                gmat[lay, 0, at, :], slab[...], dims, preferred_element_type=F32
            ) + lax.dot_general(
                gmat[lay, 1, at, :], swapped[...], dims, preferred_element_type=F32
            )
            per = block // lines
            sendbuf[step, pl.ds(b * per, per)] = total.reshape(per, lines, wide).astype(BF16)
            return 0

        lax.fori_loop(0, length // block, body, 0)

        def give(k, _):
            peer = lax.rem(me + k, count)
            remote(
                sendbuf.at[step, peer], recvbuf.at[step, me], xsend.at[step], xrecv.at[step],
                lax.rem(peer, layers), peer // layers,
            ).start()
            return 0

        lax.fori_loop(1, count, give, 0)
        recvbuf[step, me] = sendbuf[step, me]

    def arrived(step):
        most = recvbuf.at[step, pl.ds(0, count - 1)]
        remote(most, most, xsend.at[step], xrecv.at[step], sec, strip).wait_recv()
        if wide == 128:
            lane = lax.broadcasted_iota(jnp.int32, (lines, wide), 1) // lines
            for g in range(count // 4):
                pieces = [recvbuf[step, 4 * g + q].astype(F32) for q in range(4)]
                for fc in range(4):
                    out = None
                    for q in range(4):
                        shift = ((q - fc) * lines) % wide
                        moved = pltpu.roll(pieces[q], shift, axis=1) if shift else pieces[q]
                        out = moved if out is None else jnp.where(lane == q, moved, out)
                    rounded = out.astype(BF16)
                    at = slice(g * wide, (g + 1) * wide)
                    slab[fc * lines:(fc + 1) * lines, at] = rounded
                    other = fc ^ 1
                    swapped[other * lines:(other + 1) * lines, at] = (
                        rounded if fc % 2 == 0 else -rounded
                    )
        else:
            for fc in range(4):
                put(fc, jnp.concatenate(
                    [
                        recvbuf[step, d].astype(F32)[:, fc * lines:(fc + 1) * lines]
                        for d in range(count)
                    ],
                    axis=1,
                ))

    def along(lay):
        def body(b, _):
            at = pl.ds(pl.multiple_of(b * block, block), block)
            mid[:, at] = jnp.dot(
                slab[...], gmat[lay, 0, :, at], preferred_element_type=F32
            ) + jnp.dot(swapped[...], gmat[lay, 1, :, at], preferred_element_type=F32)
            return 0

        lax.fori_loop(0, length // block, body, 0)

    build(0)
    screened(0, lambda fc: launch_ref[fc, sec].astype(F32))
    across(0, 0)
    for lay in range(1, layers):
        build(lay)
    for lay in range(1, layers):
        arrived(lay - 1)
        along(lay - 1)
        screened(lay, lambda fc: mid[fc * lines:(fc + 1) * lines, :])
        across(lay, lay)
    arrived(layers - 1)
    along(layers - 1)
    for fc in range(4):
        out_ref[sec, fc] = mid[fc * lines:(fc + 1) * lines, :].astype(BF16)
    for k in range(1, layers):
        a = lax.rem(sec + k, layers)
        remote(out_ref.at[sec], out_ref.at[sec], osend, orecv, a, strip).start()
    most = out_ref.at[pl.ds(0, layers - 1)]
    remote(most, most, osend, orecv, sec, strip).wait()
    for k in range(1, layers):
        remote(g_ref, gall.at[sec], gsend, grecv.at[sec], sec, strip).wait_send()
    for lay in range(layers):
        @pl.when(sec == lay)
        def _(lay=lay):
            if lay % 2 == 0:
                some = scr_ref.at[pl.ds(0, layers - 1)]
            else:
                some = scrt_ref.at[pl.ds(0, count - 1)]
            remote(some, some, ssend, srecv.at[lay], sec, strip).wait_send()
    for step in range(layers):
        most = sendbuf.at[step, pl.ds(0, count - 1)]
        remote(most, most, xsend.at[step], xrecv.at[step], sec, strip).wait_send()


def propagate(launch, screens, line, layers, strips):
    rows, length = launch.shape[2:]
    lines = rows // layers
    count = layers * strips
    vmem = pl.BlockSpec(memory_space=pltpu.VMEM)
    dma = pltpu.SemaphoreType.DMA
    screen = screens[0]
    return pl.pallas_call(
        functools.partial(propagate_kernel, layers, strips),
        out_shape=jax.ShapeDtypeStruct((layers, 4, lines, length), BF16),
        in_specs=[vmem] * 4,
        out_specs=vmem,
        scratch_shapes=[
            pltpu.VMEM((layers, 8, length), F32),
            pltpu.VMEM((layers, 2, length, length), BF16),
            pltpu.VMEM((layers // 2, lines, length), F32),
            pltpu.VMEM((layers // 2, strips, lines, rows), F32),
            pltpu.VMEM((layers, count, lines, 4 * lines), BF16),
            pltpu.VMEM((layers, count, lines, 4 * lines), BF16),
            pltpu.VMEM((4 * lines, length), BF16),
            pltpu.VMEM((4 * lines, length), BF16),
            pltpu.VMEM((4 * lines, length), F32),
            dma, dma((layers,)), dma, dma((layers,)), dma((layers,)), dma((layers,)), dma, dma,
        ],
        compiler_params=pltpu.CompilerParams(
            collective_id=0, has_side_effects=True, vmem_limit_bytes=56 << 20
        ),
        name="propagate",
    )(
        launch.reshape(4, layers, lines, length),
        screen.reshape(layers, lines, length),
        screen.T.reshape(count, lines, rows),
        line,
    )


def per_device(launch, screens, distance, templates, send_table, send_counts):
    layers = lax.axis_size("layer")
    strips = lax.axis_size("strip")
    sec = lax.axis_index("layer")
    fields = launch.shape[0]
    rows, length = launch.shape[2:]
    line = kernel_line(distance[0], length)
    done = propagate(launch, screens, line, layers, strips)
    pupil = done.transpose(1, 0, 2, 3).reshape(fields, 2, rows, length)
    side = length // SUB
    picks = send_table[0, :, 0]
    blocks = jnp.stack([
        lax.dynamic_slice(
            pupil,
            (0, 0, picks[o] // side * SUB, picks[o] % side * SUB),
            (fields, 2, SUB, SUB),
        )
        for o in range(strips)
    ])
    flat = blocks.reshape(strips * fields, 2 * SUB * SUB)
    table = jnp.asarray(spot_table(SUB))
    pixels = templates.shape[0]
    spot = jnp.dot(flat, table, preferred_element_type=F32)
    intensity = (spot[:, :pixels] ** 2 + spot[:, pixels:] ** 2).astype(BF16)
    result = jnp.dot(intensity, templates, preferred_element_type=F32)
    result = result.reshape(strips, fields, templates.shape[1])
    live = sec < send_counts[0]
    result = jnp.where(live[:, None, None], result, 0.0)
    received = lax.all_to_all(result, "strip", split_axis=0, concat_axis=0, tiled=True)
    return (pupil, received[None, :, None])


def solution(mesh):
    placed = (
        P(None, None, "strip", None),
        P("layer", "strip", None),
        P("layer"),
        P(),
        P("strip", None, "layer"),
        P("strip", None),
    )
    return jax.shard_map(
        per_device,
        mesh=mesh,
        in_specs=placed,
        out_specs=(P(None, None, "strip", None), P("strip", None, "layer", None, None)),
        check_vma=False,
    )
```

```python
import functools
import math

import jax
import jax.numpy as jnp
import numpy as np
from jax import lax
from jax.experimental import pallas as pl
from jax.experimental.pallas import tpu as pltpu
from jax.sharding import PartitionSpec as P

SUB = 16
F32 = jnp.float32
BF16 = jnp.bfloat16
MESH = pl.DeviceIdType.MESH


def cosine_half_table(length):
    k = np.arange(length // 2, dtype=np.int64)
    n = np.arange(length, dtype=np.int64)
    p = (k[:, None] * n[None, :]) % length
    p = np.minimum(p, length - p)
    return np.cos(2.0 * np.pi * p / length).astype(np.float32).astype(BF16)


def spot_table(subsize):
    spotsize = 2 * subsize
    outer = np.arange(spotsize)
    inner = np.arange(subsize)
    angles = (inner[:, None] * outer[None, :] % spotsize) * (2.0 * np.pi / spotsize)
    wave = (np.cos(angles) - 1j * np.sin(angles)) / math.sqrt(subsize)
    kron = wave[:, None, :, None] * wave[None, :, None, :]
    kron = kron.reshape(subsize * subsize, spotsize * spotsize)
    upper = np.concatenate([kron.real, kron.imag], axis=1)
    lower = np.concatenate([-kron.imag, kron.real], axis=1)
    return np.concatenate([upper, lower], axis=0).astype(np.float32).astype(BF16)


def kernel_line(distance_value, length):
    half = length // 2
    counter = jnp.arange(half + 1, dtype=jnp.int32).astype(F32)
    phases = -distance_value * math.pi * counter * counter / float(length * length)
    h = jnp.stack([jnp.cos(phases), jnp.sin(phases)])
    weight = jnp.where(counter == 0.0, 1.0, 2.0) / length
    folded = (h * weight)[:, :half]
    high = folded.astype(BF16)
    low = (folded - high.astype(F32)).astype(BF16)
    table = jnp.asarray(cosine_half_table(length))
    parts = jnp.dot(jnp.concatenate([high, low]), table, preferred_element_type=F32)
    sign = (1 - 2 * (jnp.arange(length, dtype=jnp.int32) % 2)).astype(F32) / length
    line = parts[:2] + parts[2:] + h[:, half:] * sign
    return jnp.concatenate([line, jnp.zeros((6, length), F32)])


def sincos(x):
    y = 0.5 * x
    z = y * y
    s = -1.0 / 39916800.0
    for c in (1.0 / 362880.0, -1.0 / 5040.0, 1.0 / 120.0, -1.0 / 6.0, 1.0):
        s = s * z + c
    s = s * y
    c0 = 1.0 / 479001600.0
    for c in (-1.0 / 3628800.0, 1.0 / 40320.0, -1.0 / 720.0, 1.0 / 24.0, -0.5, 1.0):
        c0 = c0 * z + c
    return 2.0 * s * c0, 1.0 - 2.0 * s * s


def propagate_kernel(
    layers, strips, launch_ref, scr_ref, scrt_ref, g_ref, out_ref,
    gall, gmat, srow, scol, sendbuf, recvbuf, slab, swapped, mid,
    gsend, grecv, ssend, srecv, xsend, xrecv, osend, orecv,
):
    count = layers * strips
    length = launch_ref.shape[-1]
    lines = launch_ref.shape[-2]
    wide = 4 * lines
    sec = lax.axis_index("layer")
    strip = lax.axis_index("strip")
    me = strip * layers + sec

    barrier = pltpu.get_barrier_semaphore()

    def greet(k, _):
        peer = lax.rem(me + k, count)
        pl.semaphore_signal(
            barrier, inc=1, device_id=(lax.rem(peer, layers), peer // layers), device_id_type=MESH
        )
        return 0

    lax.fori_loop(1, count, greet, 0)
    pl.semaphore_wait(barrier, count - 1)

    def remote(src, dst, ssem, rsem, a, s):
        return pltpu.make_async_remote_copy(
            src_ref=src, dst_ref=dst, send_sem=ssem, recv_sem=rsem,
            device_id=(a, s), device_id_type=MESH,
        )

    for k in range(1, layers):
        a = lax.rem(sec + k, layers)
        remote(g_ref, gall.at[sec], gsend, grecv.at[sec], a, strip).start()
    for lay in range(layers):
        if lay % 2 == 0:
            @pl.when(sec == lay)
            def _(lay=lay):
                for k in range(1, layers):
                    a = lax.rem(sec + k, layers)
                    remote(scr_ref.at[a], srow.at[lay // 2], ssend, srecv.at[lay], a, strip).start()
                srow[lay // 2] = scr_ref[lay]
        else:
            @pl.when(sec == lay)
            def _(lay=lay):
                def give(k, _):
                    peer = lax.rem(me + k, count)
                    remote(
                        scrt_ref.at[peer], scol.at[lay // 2, strip], ssend, srecv.at[lay],
                        lax.rem(peer, layers), peer // layers,
                    ).start()
                    return 0

                lax.fori_loop(1, count, give, 0)
                scol[lay // 2, strip] = scrt_ref[me]
    gall[sec] = g_ref[...]

    def build(lay):
        @pl.when(sec != lay)
        def _():
            remote(g_ref, gall.at[lay], gsend, grecv.at[lay], sec, strip).wait_recv()

        band = 128
        for part in range(2):
            row = gall[lay, part:part + 1, :]
            base = pltpu.roll(
                jnp.broadcast_to(row, (band, length)), 0, axis=1, stride=1, stride_axis=0
            ).astype(BF16)
            for b in range(length // band):
                at = band * b
                if b:
                    gmat[lay, part, at:at + band, 0:at] = base[:, length - at:]
                gmat[lay, part, at:at + band, at:] = base[:, :length - at]

    def screen_of(lay):
        if lay % 2 == 0:
            @pl.when(sec != lay)
            def _():
                remote(scr_ref.at[0], srow.at[lay // 2], ssend, srecv.at[lay], sec, strip).wait_recv()
            return sincos(srow[lay // 2])

        @pl.when(sec != lay)
        def _():
            whole = scol.at[lay // 2]
            remote(whole, whole, ssend, srecv.at[lay], sec, strip).wait_recv()

        @pl.when(sec == lay)
        def _():
            most = scol.at[lay // 2, pl.ds(0, strips - 1)]
            remote(most, most, ssend, srecv.at[lay], sec, strip).wait_recv()

        theta = jnp.concatenate([scol[lay // 2, s] for s in range(strips)], axis=1)
        return sincos(theta)

    def put(fc, value):
        rounded = value.astype(BF16)
        slab[fc * lines:(fc + 1) * lines, :] = rounded
        other = fc ^ 1
        swapped[other * lines:(other + 1) * lines, :] = rounded if fc % 2 == 0 else -rounded

    def screened(lay, load):
        sine, cosine = screen_of(lay)
        for f in range(2):
            re = load(2 * f)
            im = load(2 * f + 1)
            put(2 * f, re * cosine - im * sine)
            put(2 * f + 1, re * sine + im * cosine)

    block = 256

    def across(lay, step):
        def body(b, _):
            at = pl.ds(pl.multiple_of(b * block, block), block)
            dims = (((1,), (1,)), ((), ()))
            total = lax.dot_general(
                gmat[lay, 0, at, :], slab[...], dims, preferred_element_type=F32
            ) + lax.dot_general(
                gmat[lay, 1, at, :], swapped[...], dims, preferred_element_type=F32
            )
            per = block // lines
            sendbuf[step, pl.ds(b * per, per)] = total.reshape(per, lines, wide).astype(BF16)
            return 0

        lax.fori_loop(0, length // block, body, 0)

        def give(k, _):
            peer = lax.rem(me + k, count)
            remote(
                sendbuf.at[step, peer], recvbuf.at[step, me], xsend.at[step], xrecv.at[step],
                lax.rem(peer, layers), peer // layers,
            ).start()
            return 0

        lax.fori_loop(1, count, give, 0)
        recvbuf[step, me] = sendbuf[step, me]

    def arrived(step):
        most = recvbuf.at[step, pl.ds(0, count - 1)]
        remote(most, most, xsend.at[step], xrecv.at[step], sec, strip).wait_recv()
        if wide == 128:
            lane = lax.broadcasted_iota(jnp.int32, (lines, wide), 1) // lines
            for g in range(count // 4):
                pieces = [recvbuf[step, 4 * g + q].astype(F32) for q in range(4)]
                for fc in range(4):
                    out = None
                    for q in range(4):
                        shift = ((q - fc) * lines) % wide
                        moved = pltpu.roll(pieces[q], shift, axis=1) if shift else pieces[q]
                        out = moved if out is None else jnp.where(lane == q, moved, out)
                    rounded = out.astype(BF16)
                    at = slice(g * wide, (g + 1) * wide)
                    slab[fc * lines:(fc + 1) * lines, at] = rounded
                    other = fc ^ 1
                    swapped[other * lines:(other + 1) * lines, at] = (
                        rounded if fc % 2 == 0 else -rounded
                    )
        else:
            for fc in range(4):
                put(fc, jnp.concatenate(
                    [
                        recvbuf[step, d].astype(F32)[:, fc * lines:(fc + 1) * lines]
                        for d in range(count)
                    ],
                    axis=1,
                ))

    def along(lay):
        def body(b, _):
            at = pl.ds(pl.multiple_of(b * block, block), block)
            mid[:, at] = jnp.dot(
                slab[...], gmat[lay, 0, :, at], preferred_element_type=F32
            ) + jnp.dot(swapped[...], gmat[lay, 1, :, at], preferred_element_type=F32)
            return 0

        lax.fori_loop(0, length // block, body, 0)

    build(0)
    screened(0, lambda fc: launch_ref[fc, sec].astype(F32))
    across(0, 0)
    for lay in range(1, layers):
        build(lay)
    for lay in range(1, layers):
        arrived(lay - 1)
        along(lay - 1)
        screened(lay, lambda fc: mid[fc * lines:(fc + 1) * lines, :])
        across(lay, lay)
    arrived(layers - 1)
    along(layers - 1)
    for fc in range(4):
        out_ref[sec, fc] = mid[fc * lines:(fc + 1) * lines, :].astype(BF16)
    for k in range(1, layers):
        a = lax.rem(sec + k, layers)
        remote(out_ref.at[sec], out_ref.at[sec], osend, orecv, a, strip).start()
    most = out_ref.at[pl.ds(0, layers - 1)]
    remote(most, most, osend, orecv, sec, strip).wait()
    for k in range(1, layers):
        remote(g_ref, gall.at[sec], gsend, grecv.at[sec], sec, strip).wait_send()
    for lay in range(layers):
        @pl.when(sec == lay)
        def _(lay=lay):
            if lay % 2 == 0:
                some = scr_ref.at[pl.ds(0, layers - 1)]
            else:
                some = scrt_ref.at[pl.ds(0, count - 1)]
            remote(some, some, ssend, srecv.at[lay], sec, strip).wait_send()
    for step in range(layers):
        most = sendbuf.at[step, pl.ds(0, count - 1)]
        remote(most, most, xsend.at[step], xrecv.at[step], sec, strip).wait_send()


def propagate(launch, screens, line, layers, strips):
    rows, length = launch.shape[2:]
    lines = rows // layers
    count = layers * strips
    vmem = pl.BlockSpec(memory_space=pltpu.VMEM)
    dma = pltpu.SemaphoreType.DMA
    screen = screens[0]
    return pl.pallas_call(
        functools.partial(propagate_kernel, layers, strips),
        out_shape=jax.ShapeDtypeStruct((layers, 4, lines, length), BF16),
        in_specs=[vmem] * 4,
        out_specs=vmem,
        scratch_shapes=[
            pltpu.VMEM((layers, 8, length), F32),
            pltpu.VMEM((layers, 2, length, length), BF16),
            pltpu.VMEM((layers // 2, lines, length), F32),
            pltpu.VMEM((layers // 2, strips, lines, rows), F32),
            pltpu.VMEM((layers, count, lines, 4 * lines), BF16),
            pltpu.VMEM((layers, count, lines, 4 * lines), BF16),
            pltpu.VMEM((4 * lines, length), BF16),
            pltpu.VMEM((4 * lines, length), BF16),
            pltpu.VMEM((4 * lines, length), F32),
            dma, dma((layers,)), dma, dma((layers,)), dma((layers,)), dma((layers,)), dma, dma,
        ],
        compiler_params=pltpu.CompilerParams(
            collective_id=0, has_side_effects=True, vmem_limit_bytes=56 << 20
        ),
        name="propagate",
    )(
        launch.reshape(4, layers, lines, length),
        screen.reshape(layers, lines, length),
        screen.T.reshape(count, lines, rows),
        line,
    )


def gather_kernel(side, picks_ref, pupil_ref, out_ref):
    for o in range(out_ref.shape[0]):
        pick = picks_ref[o]
        top = pl.multiple_of(pick // side * SUB, SUB)
        left = pick % side * SUB
        tile = pl.multiple_of(left // 128 * 128, 128)
        shift = (128 - left % 128) % 128
        for part in range(4):
            rows = pupil_ref[part, pl.ds(top, SUB), pl.ds(tile, 128)].astype(F32)
            out_ref[o, part] = pltpu.roll(rows, shift, axis=1)[:, :SUB].astype(BF16)


def gather_blocks(pupil, picks):
    vmem = pl.BlockSpec(memory_space=pltpu.VMEM)
    return pl.pallas_call(
        functools.partial(gather_kernel, pupil.shape[-1] // SUB),
        out_shape=jax.ShapeDtypeStruct((picks.shape[0], 4, SUB, SUB), BF16),
        in_specs=[pl.BlockSpec(memory_space=pltpu.SMEM), vmem],
        out_specs=vmem,
        name="gather",
    )(picks, pupil)


def swap_kernel(strips, in_ref, out_ref, send, recv):
    sec = lax.axis_index("layer")
    strip = lax.axis_index("strip")
    barrier = pltpu.get_barrier_semaphore()
    for k in range(1, strips):
        pl.semaphore_signal(
            barrier, inc=1, device_id=(sec, lax.rem(strip + k, strips)), device_id_type=MESH
        )
    pl.semaphore_wait(barrier, strips - 1)
    for k in range(1, strips):
        peer = lax.rem(strip + k, strips)
        pltpu.make_async_remote_copy(
            src_ref=in_ref.at[peer], dst_ref=out_ref.at[strip], send_sem=send, recv_sem=recv,
            device_id=(sec, peer), device_id_type=MESH,
        ).start()
    out_ref[strip] = in_ref[strip]
    most = out_ref.at[pl.ds(0, strips - 1)]
    pltpu.make_async_remote_copy(
        src_ref=most, dst_ref=most, send_sem=send, recv_sem=recv,
        device_id=(sec, strip), device_id_type=MESH,
    ).wait()


def swap_strips(result, strips):
    fields, channels = result.shape[1:]
    vmem = pl.BlockSpec(memory_space=pltpu.VMEM)
    dma = pltpu.SemaphoreType.DMA
    out = pl.pallas_call(
        functools.partial(swap_kernel, strips),
        out_shape=jax.ShapeDtypeStruct((strips, 8, 128), F32),
        in_specs=[vmem],
        out_specs=vmem,
        scratch_shapes=[dma, dma],
        compiler_params=pltpu.CompilerParams(collective_id=1, has_side_effects=True),
        name="swap",
    )(jnp.pad(result, ((0, 0), (0, 8 - fields), (0, 128 - channels))))
    return out[:, :fields, :channels]


def per_device(launch, screens, distance, templates, send_table, send_counts):
    layers = lax.axis_size("layer")
    strips = lax.axis_size("strip")
    sec = lax.axis_index("layer")
    fields = launch.shape[0]
    rows, length = launch.shape[2:]
    line = kernel_line(distance[0], length)
    done = propagate(launch, screens, line, layers, strips)
    pupil = done.transpose(1, 0, 2, 3).reshape(fields, 2, rows, length)
    side = length // SUB
    blocks = gather_blocks(pupil.reshape(2 * fields, rows, length), send_table.reshape(strips))
    flat = blocks.reshape(strips * fields, 2 * SUB * SUB)
    table = jnp.asarray(spot_table(SUB))
    pixels = templates.shape[0]
    spot = jnp.dot(flat, table, preferred_element_type=F32)
    intensity = (spot[:, :pixels] ** 2 + spot[:, pixels:] ** 2).astype(BF16)
    result = jnp.dot(intensity, templates, preferred_element_type=F32)
    result = result.reshape(strips, fields, templates.shape[1])
    live = sec < send_counts[0]
    result = jnp.where(live[:, None, None], result, 0.0)
    received = swap_strips(result, strips)
    return (pupil, received[None, :, None])


def solution(mesh):
    placed = (
        P(None, None, "strip", None),
        P("layer", "strip", None),
        P("layer"),
        P(),
        P("strip", None, "layer"),
        P("strip", None),
    )
    return jax.shard_map(
        per_device,
        mesh=mesh,
        in_specs=placed,
        out_specs=(P(None, None, "strip", None), P("strip", None, "layer", None, None)),
        check_vma=False,
    )
```

```python
import functools
import math

import jax
import jax.numpy as jnp
import numpy as np
from jax import lax
from jax.experimental import pallas as pl
from jax.experimental.pallas import tpu as pltpu
from jax.sharding import PartitionSpec as P

SUB = 16
F32 = jnp.float32
BF16 = jnp.bfloat16
MESH = pl.DeviceIdType.MESH


def cosine_half_table(length):
    k = np.arange(length // 2, dtype=np.int64)
    n = np.arange(length, dtype=np.int64)
    p = (k[:, None] * n[None, :]) % length
    p = np.minimum(p, length - p)
    return np.cos(2.0 * np.pi * p / length).astype(np.float32).astype(BF16)


def spot_table(subsize):
    spotsize = 2 * subsize
    outer = np.arange(spotsize)
    inner = np.arange(subsize)
    angles = (inner[:, None] * outer[None, :] % spotsize) * (2.0 * np.pi / spotsize)
    wave = (np.cos(angles) - 1j * np.sin(angles)) / math.sqrt(subsize)
    kron = wave[:, None, :, None] * wave[None, :, None, :]
    kron = kron.reshape(subsize * subsize, spotsize * spotsize)
    upper = np.concatenate([kron.real, kron.imag], axis=1)
    lower = np.concatenate([-kron.imag, kron.real], axis=1)
    return np.concatenate([upper, lower], axis=0).astype(np.float32).astype(BF16)


def kernel_line(distance_value, length):
    half = length // 2
    counter = jnp.arange(half + 1, dtype=jnp.int32).astype(F32)
    phases = -distance_value * math.pi * counter * counter / float(length * length)
    h = jnp.stack([jnp.cos(phases), jnp.sin(phases)])
    weight = jnp.where(counter == 0.0, 1.0, 2.0) / length
    folded = (h * weight)[:, :half]
    high = folded.astype(BF16)
    low = (folded - high.astype(F32)).astype(BF16)
    table = jnp.asarray(cosine_half_table(length))
    parts = jnp.dot(jnp.concatenate([high, low]), table, preferred_element_type=F32)
    sign = (1 - 2 * (jnp.arange(length, dtype=jnp.int32) % 2)).astype(F32) / length
    line = parts[:2] + parts[2:] + h[:, half:] * sign
    return jnp.concatenate([line, jnp.zeros((6, length), F32)])


def sincos(x):
    y = 0.5 * x
    z = y * y
    s = -1.0 / 39916800.0
    for c in (1.0 / 362880.0, -1.0 / 5040.0, 1.0 / 120.0, -1.0 / 6.0, 1.0):
        s = s * z + c
    s = s * y
    c0 = 1.0 / 479001600.0
    for c in (-1.0 / 3628800.0, 1.0 / 40320.0, -1.0 / 720.0, 1.0 / 24.0, -0.5, 1.0):
        c0 = c0 * z + c
    return 2.0 * s * c0, 1.0 - 2.0 * s * s


def propagate_kernel(
    layers, strips, launch_ref, scr_ref, scrt_ref, g_ref, out_ref,
    gall, gmat, early_row, early_col, stage_row, stage_col, srow, scol, sendbuf, recvbuf, slab, swapped, mid,
    gsend, grecv, ssend, srecv, xsend, xrecv, osend, orecv,
):
    count = layers * strips
    length = launch_ref.shape[-1]
    lines = launch_ref.shape[-2]
    wide = 4 * lines
    sec = lax.axis_index("layer")
    strip = lax.axis_index("strip")
    me = strip * layers + sec

    barrier = pltpu.get_barrier_semaphore()

    def greet(k, _):
        peer = lax.rem(me + k, count)
        pl.semaphore_signal(
            barrier, inc=1, device_id=(lax.rem(peer, layers), peer // layers), device_id_type=MESH
        )
        return 0

    lax.fori_loop(1, count, greet, 0)
    pl.semaphore_wait(barrier, count - 1)

    def remote(src, dst, ssem, rsem, a, s):
        return pltpu.make_async_remote_copy(
            src_ref=src, dst_ref=dst, send_sem=ssem, recv_sem=rsem,
            device_id=(a, s), device_id_type=MESH,
        )

    for k in range(1, layers):
        a = lax.rem(sec + k, layers)
        remote(g_ref, gall.at[sec], gsend, grecv.at[sec], a, strip).start()
    def to_all(start_one):
        half = strips // 2

        def far(i, _):
            other = lax.rem(strip // half + 1, 2) * half + lax.rem(strip + i // layers, half)
            start_one(lax.rem(sec + i, layers), other)
            return 0

        def near(i, _):
            other = strip // half * half + lax.rem(strip + i // layers, half)
            start_one(lax.rem(sec + i, layers), other)
            return 0

        lax.fori_loop(0, half * layers, far, 0)
        lax.fori_loop(1, half * layers, near, 0)

    rows_of = [(stage_row, early_row)] + [(scr_ref, srow.at[i]) for i in range(layers // 2 - 1)]
    cols_of = [(stage_col, early_col)] + [(scrt_ref, scol.at[i]) for i in range(layers // 2 - 1)]

    def share(lay):
        @pl.when(sec == lay)
        def _():
            if lay % 2 == 0:
                src, dst = rows_of[lay // 2]
                if lay < 2:
                    src[...] = scr_ref[...].astype(BF16)
                for k in range(1, layers):
                    a = lax.rem(sec + k, layers)
                    remote(src.at[a], dst, ssend, srecv.at[lay], a, strip).start()
                dst[...] = src[lay]
            else:
                src, dst = cols_of[lay // 2]
                if lay < 2:
                    src[...] = scrt_ref[...].astype(BF16)

                def one(a, s):
                    remote(
                        src.at[s * layers + a], dst.at[strip], ssend, srecv.at[lay], a, s
                    ).start()

                to_all(one)
                dst[strip] = src[me]

    for lay in range(2):
        share(lay)
    gall[sec] = g_ref[...]

    def build(lay):
        @pl.when(sec != lay)
        def _():
            remote(g_ref, gall.at[lay], gsend, grecv.at[lay], sec, strip).wait_recv()

        band = 128
        for part in range(2):
            row = gall[lay, part:part + 1, :]
            base = pltpu.roll(
                jnp.broadcast_to(row, (band, length)), 0, axis=1, stride=1, stride_axis=0
            ).astype(BF16)
            for b in range(length // band):
                at = band * b
                if b:
                    gmat[lay, part, at:at + band, 0:at] = base[:, length - at:]
                gmat[lay, part, at:at + band, at:] = base[:, :length - at]

    def screen_of(lay):
        if lay % 2 == 0:
            src, dst = rows_of[lay // 2]

            @pl.when(sec != lay)
            def _():
                remote(src.at[0], dst, ssend, srecv.at[lay], sec, strip).wait_recv()
            return sincos(dst[...].astype(F32))

        dst = cols_of[lay // 2][1]

        @pl.when(sec != lay)
        def _():
            remote(dst, dst, ssend, srecv.at[lay], sec, strip).wait_recv()

        @pl.when(sec == lay)
        def _():
            most = dst.at[pl.ds(0, strips - 1)]
            remote(most, most, ssend, srecv.at[lay], sec, strip).wait_recv()

        return sincos(jnp.concatenate([dst[s].astype(F32) for s in range(strips)], axis=1))

    def put(fc, value):
        rounded = value.astype(BF16)
        slab[fc * lines:(fc + 1) * lines, :] = rounded
        other = fc ^ 1
        swapped[other * lines:(other + 1) * lines, :] = rounded if fc % 2 == 0 else -rounded

    def screened(lay, load):
        sine, cosine = screen_of(lay)
        for f in range(2):
            re = load(2 * f)
            im = load(2 * f + 1)
            put(2 * f, re * cosine - im * sine)
            put(2 * f + 1, re * sine + im * cosine)

    block = 256

    def across(lay, step):
        def body(b, _):
            at = pl.ds(pl.multiple_of(b * block, block), block)
            dims = (((1,), (1,)), ((), ()))
            total = lax.dot_general(
                gmat[lay, 0, at, :], slab[...], dims, preferred_element_type=F32
            ) + lax.dot_general(
                gmat[lay, 1, at, :], swapped[...], dims, preferred_element_type=F32
            )
            per = block // lines
            sendbuf[step, pl.ds(b * per, per)] = total.reshape(per, lines, wide).astype(BF16)
            return 0

        lax.fori_loop(0, length // block, body, 0)

        def one(a, s):
            remote(
                sendbuf.at[step, s * layers + a], recvbuf.at[step, me],
                xsend.at[step], xrecv.at[step], a, s,
            ).start()

        to_all(one)
        recvbuf[step, me] = sendbuf[step, me]

    def arrived(step):
        most = recvbuf.at[step, pl.ds(0, count - 1)]
        remote(most, most, xsend.at[step], xrecv.at[step], sec, strip).wait_recv()
        if wide == 128:
            lane = lax.broadcasted_iota(jnp.int32, (lines, wide), 1) // lines
            for g in range(count // 4):
                pieces = [recvbuf[step, 4 * g + q].astype(F32) for q in range(4)]
                for fc in range(4):
                    out = None
                    for q in range(4):
                        shift = ((q - fc) * lines) % wide
                        moved = pltpu.roll(pieces[q], shift, axis=1) if shift else pieces[q]
                        out = moved if out is None else jnp.where(lane == q, moved, out)
                    rounded = out.astype(BF16)
                    at = slice(g * wide, (g + 1) * wide)
                    slab[fc * lines:(fc + 1) * lines, at] = rounded
                    other = fc ^ 1
                    swapped[other * lines:(other + 1) * lines, at] = (
                        rounded if fc % 2 == 0 else -rounded
                    )
        else:
            for fc in range(4):
                put(fc, jnp.concatenate(
                    [
                        recvbuf[step, d].astype(F32)[:, fc * lines:(fc + 1) * lines]
                        for d in range(count)
                    ],
                    axis=1,
                ))

    def along(lay):
        def body(b, _):
            at = pl.ds(pl.multiple_of(b * block, block), block)
            mid[:, at] = jnp.dot(
                slab[...], gmat[lay, 0, :, at], preferred_element_type=F32
            ) + jnp.dot(swapped[...], gmat[lay, 1, :, at], preferred_element_type=F32)
            return 0

        lax.fori_loop(0, length // block, body, 0)

    build(0)
    screened(0, lambda fc: launch_ref[fc, sec].astype(F32))
    across(0, 0)
    for lay in range(1, layers):
        build(lay)
    for lay in range(1, layers):
        arrived(lay - 1)
        if lay == 1:
            for late in range(2, layers):
                share(late)
        along(lay - 1)
        screened(lay, lambda fc: mid[fc * lines:(fc + 1) * lines, :])
        across(lay, lay)
    arrived(layers - 1)
    along(layers - 1)
    for fc in range(4):
        out_ref[sec, fc] = mid[fc * lines:(fc + 1) * lines, :].astype(BF16)
    for k in range(1, layers):
        a = lax.rem(sec + k, layers)
        remote(out_ref.at[sec], out_ref.at[sec], osend, orecv, a, strip).start()
    most = out_ref.at[pl.ds(0, layers - 1)]
    remote(most, most, osend, orecv, sec, strip).wait()
    for k in range(1, layers):
        remote(g_ref, gall.at[sec], gsend, grecv.at[sec], sec, strip).wait_send()
    for lay in range(layers):
        @pl.when(sec == lay)
        def _(lay=lay):
            if lay % 2 == 0:
                some = rows_of[lay // 2][0].at[pl.ds(0, layers - 1)]
            else:
                some = cols_of[lay // 2][0].at[pl.ds(0, count - 1)]
            remote(some, some, ssend, srecv.at[lay], sec, strip).wait_send()
    for step in range(layers):
        most = sendbuf.at[step, pl.ds(0, count - 1)]
        remote(most, most, xsend.at[step], xrecv.at[step], sec, strip).wait_send()


def propagate(launch, screens, line, layers, strips):
    rows, length = launch.shape[2:]
    lines = rows // layers
    count = layers * strips
    vmem = pl.BlockSpec(memory_space=pltpu.VMEM)
    dma = pltpu.SemaphoreType.DMA
    screen = screens[0]
    return pl.pallas_call(
        functools.partial(propagate_kernel, layers, strips),
        out_shape=jax.ShapeDtypeStruct((layers, 4, lines, length), BF16),
        in_specs=[vmem] * 4,
        out_specs=vmem,
        scratch_shapes=[
            pltpu.VMEM((layers, 8, length), F32),
            pltpu.VMEM((layers, 2, length, length), BF16),
            pltpu.VMEM((lines, length), BF16),
            pltpu.VMEM((strips, lines, rows), BF16),
            pltpu.VMEM((layers, lines, length), BF16),
            pltpu.VMEM((count, lines, rows), BF16),
            pltpu.VMEM((layers // 2 - 1, lines, length), F32),
            pltpu.VMEM((layers // 2 - 1, strips, lines, rows), F32),
            pltpu.VMEM((layers, count, lines, 4 * lines), BF16),
            pltpu.VMEM((layers, count, lines, 4 * lines), BF16),
            pltpu.VMEM((4 * lines, length), BF16),
            pltpu.VMEM((4 * lines, length), BF16),
            pltpu.VMEM((4 * lines, length), F32),
            dma, dma((layers,)), dma, dma((layers,)), dma((layers,)), dma((layers,)), dma, dma,
        ],
        compiler_params=pltpu.CompilerParams(
            collective_id=0, has_side_effects=True, vmem_limit_bytes=56 << 20
        ),
        name="propagate",
    )(
        launch.reshape(4, layers, lines, length),
        screen.reshape(layers, lines, length),
        screen.T.reshape(count, lines, rows),
        line,
    )


def gather_kernel(side, picks_ref, pupil_ref, out_ref):
    for o in range(out_ref.shape[0]):
        pick = picks_ref[o]
        top = pl.multiple_of(pick // side * SUB, SUB)
        left = pick % side * SUB
        tile = pl.multiple_of(left // 128 * 128, 128)
        shift = (128 - left % 128) % 128
        for part in range(4):
            rows = pupil_ref[part, pl.ds(top, SUB), pl.ds(tile, 128)].astype(F32)
            out_ref[o, part] = pltpu.roll(rows, shift, axis=1)[:, :SUB].astype(BF16)


def gather_blocks(pupil, picks):
    vmem = pl.BlockSpec(memory_space=pltpu.VMEM)
    return pl.pallas_call(
        functools.partial(gather_kernel, pupil.shape[-1] // SUB),
        out_shape=jax.ShapeDtypeStruct((picks.shape[0], 4, SUB, SUB), BF16),
        in_specs=[pl.BlockSpec(memory_space=pltpu.SMEM), vmem],
        out_specs=vmem,
        name="gather",
    )(picks, pupil)


def swap_kernel(strips, in_ref, out_ref, send, recv):
    sec = lax.axis_index("layer")
    strip = lax.axis_index("strip")
    barrier = pltpu.get_barrier_semaphore()
    for k in range(1, strips):
        pl.semaphore_signal(
            barrier, inc=1, device_id=(sec, lax.rem(strip + k, strips)), device_id_type=MESH
        )
    pl.semaphore_wait(barrier, strips - 1)
    for k in range(1, strips):
        peer = lax.rem(strip + k, strips)
        pltpu.make_async_remote_copy(
            src_ref=in_ref.at[peer], dst_ref=out_ref.at[strip], send_sem=send, recv_sem=recv,
            device_id=(sec, peer), device_id_type=MESH,
        ).start()
    out_ref[strip] = in_ref[strip]
    most = out_ref.at[pl.ds(0, strips - 1)]
    pltpu.make_async_remote_copy(
        src_ref=most, dst_ref=most, send_sem=send, recv_sem=recv,
        device_id=(sec, strip), device_id_type=MESH,
    ).wait()


def swap_strips(result, strips):
    fields, channels = result.shape[1:]
    vmem = pl.BlockSpec(memory_space=pltpu.VMEM)
    dma = pltpu.SemaphoreType.DMA
    out = pl.pallas_call(
        functools.partial(swap_kernel, strips),
        out_shape=jax.ShapeDtypeStruct((strips, 8, 128), F32),
        in_specs=[vmem],
        out_specs=vmem,
        scratch_shapes=[dma, dma],
        compiler_params=pltpu.CompilerParams(collective_id=1, has_side_effects=True),
        name="swap",
    )(jnp.pad(result, ((0, 0), (0, 8 - fields), (0, 128 - channels))))
    return out[:, :fields, :channels]


def per_device(launch, screens, distance, templates, send_table, send_counts):
    layers = lax.axis_size("layer")
    strips = lax.axis_size("strip")
    sec = lax.axis_index("layer")
    fields = launch.shape[0]
    rows, length = launch.shape[2:]
    line = kernel_line(distance[0], length)
    done = propagate(launch, screens, line, layers, strips)
    pupil = done.transpose(1, 0, 2, 3).reshape(fields, 2, rows, length)
    side = length // SUB
    blocks = gather_blocks(pupil.reshape(2 * fields, rows, length), send_table.reshape(strips))
    flat = blocks.reshape(strips * fields, 2 * SUB * SUB)
    table = jnp.asarray(spot_table(SUB))
    pixels = templates.shape[0]
    spot = jnp.dot(flat, table, preferred_element_type=F32)
    intensity = (spot[:, :pixels] ** 2 + spot[:, pixels:] ** 2).astype(BF16)
    result = jnp.dot(intensity, templates, preferred_element_type=F32)
    result = result.reshape(strips, fields, templates.shape[1])
    live = sec < send_counts[0]
    result = jnp.where(live[:, None, None], result, 0.0)
    received = swap_strips(result, strips)
    return (pupil, received[None, :, None])


def solution(mesh):
    placed = (
        P(None, None, "strip", None),
        P("layer", "strip", None),
        P("layer"),
        P(),
        P("strip", None, "layer"),
        P("strip", None),
    )
    return jax.shard_map(
        per_device,
        mesh=mesh,
        in_specs=placed,
        out_specs=(P(None, None, "strip", None), P("strip", None, "layer", None, None)),
        check_vma=False,
    )
```

```python
import functools
import math

import jax
import jax.numpy as jnp
import numpy as np
from jax import lax
from jax.experimental import pallas as pl
from jax.experimental.pallas import tpu as pltpu
from jax.sharding import PartitionSpec as P

SUB = 16
F32 = jnp.float32
BF16 = jnp.bfloat16
MESH = pl.DeviceIdType.MESH


def cosine_half_table(length):
    k = np.arange(length // 2, dtype=np.int64)
    n = np.arange(length, dtype=np.int64)
    p = (k[:, None] * n[None, :]) % length
    p = np.minimum(p, length - p)
    return np.cos(2.0 * np.pi * p / length).astype(np.float32).astype(BF16)


def spot_table(subsize):
    spotsize = 2 * subsize
    outer = np.arange(spotsize)
    inner = np.arange(subsize)
    angles = (inner[:, None] * outer[None, :] % spotsize) * (2.0 * np.pi / spotsize)
    wave = (np.cos(angles) - 1j * np.sin(angles)) / math.sqrt(subsize)
    kron = wave[:, None, :, None] * wave[None, :, None, :]
    kron = kron.reshape(subsize * subsize, spotsize * spotsize)
    upper = np.concatenate([kron.real, kron.imag], axis=1)
    lower = np.concatenate([-kron.imag, kron.real], axis=1)
    return np.concatenate([upper, lower], axis=0).astype(np.float32).astype(BF16)


def kernel_line(distance_value, length):
    half = length // 2
    counter = jnp.arange(half + 1, dtype=jnp.int32).astype(F32)
    phases = -distance_value * math.pi * counter * counter / float(length * length)
    h = jnp.stack([jnp.cos(phases), jnp.sin(phases)])
    weight = jnp.where(counter == 0.0, 1.0, 2.0) / length
    folded = (h * weight)[:, :half]
    high = folded.astype(BF16)
    low = (folded - high.astype(F32)).astype(BF16)
    table = jnp.asarray(cosine_half_table(length))
    parts = jnp.dot(jnp.concatenate([high, low]), table, preferred_element_type=F32)
    sign = (1 - 2 * (jnp.arange(length, dtype=jnp.int32) % 2)).astype(F32) / length
    line = parts[:2] + parts[2:] + h[:, half:] * sign
    return jnp.concatenate([line, jnp.zeros((6, length), F32)])


def sincos(x):
    y = 0.5 * x
    z = y * y
    s = -1.0 / 39916800.0
    for c in (1.0 / 362880.0, -1.0 / 5040.0, 1.0 / 120.0, -1.0 / 6.0, 1.0):
        s = s * z + c
    s = s * y
    c0 = 1.0 / 479001600.0
    for c in (-1.0 / 3628800.0, 1.0 / 40320.0, -1.0 / 720.0, 1.0 / 24.0, -0.5, 1.0):
        c0 = c0 * z + c
    return 2.0 * s * c0, 1.0 - 2.0 * s * s


def propagate_kernel(
    layers, strips, launch_ref, scr_ref, scrt_ref, g_ref, out_ref,
    gall, gmat, early_row, early_col, stage_row, stage_col, srow, scol, sendbuf, recvbuf, slab, swapped, mid,
    gsend, grecv, ssend, srecv, xsend, xrecv, osend, orecv,
):
    count = layers * strips
    length = launch_ref.shape[-1]
    lines = launch_ref.shape[-2]
    wide = 4 * lines
    sec = lax.axis_index("layer")
    strip = lax.axis_index("strip")
    me = strip * layers + sec

    barrier = pltpu.get_barrier_semaphore()

    def greet(k, _):
        peer = lax.rem(me + k, count)
        pl.semaphore_signal(
            barrier, inc=1, device_id=(lax.rem(peer, layers), peer // layers), device_id_type=MESH
        )
        return 0

    lax.fori_loop(1, count, greet, 0)
    pl.semaphore_wait(barrier, count - 1)

    def remote(src, dst, ssem, rsem, a, s):
        return pltpu.make_async_remote_copy(
            src_ref=src, dst_ref=dst, send_sem=ssem, recv_sem=rsem,
            device_id=(a, s), device_id_type=MESH,
        )

    for k in range(1, layers):
        a = lax.rem(sec + k, layers)
        remote(g_ref, gall.at[sec], gsend, grecv.at[sec], a, strip).start()
    def to_all(start_one):
        def one(k, _):
            peer = lax.rem(me + k, count)
            start_one(lax.rem(peer, layers), peer // layers)
            return 0

        lax.fori_loop(1, count, one, 0)

    rows_of = [(stage_row, early_row)] + [(scr_ref, srow.at[i]) for i in range(layers // 2 - 1)]
    cols_of = [(stage_col, early_col)] + [(scrt_ref, scol.at[i]) for i in range(layers // 2 - 1)]

    def share(lay):
        @pl.when(sec == lay)
        def _():
            if lay % 2 == 0:
                src, dst = rows_of[lay // 2]
                if lay < 2:
                    src[...] = scr_ref[...].astype(BF16)
                for k in range(1, layers):
                    a = lax.rem(sec + k, layers)
                    remote(src.at[a], dst, ssend, srecv.at[lay], a, strip).start()
                dst[...] = src[lay]
            else:
                src, dst = cols_of[lay // 2]
                if lay < 2:
                    src[...] = scrt_ref[...].astype(BF16)

                def one(a, s):
                    remote(
                        src.at[s * layers + a], dst.at[strip], ssend, srecv.at[lay], a, s
                    ).start()

                to_all(one)
                dst[strip] = src[me]

    for lay in range(layers):
        share(lay)
    gall[sec] = g_ref[...]

    def build(lay):
        @pl.when(sec != lay)
        def _():
            remote(g_ref, gall.at[lay], gsend, grecv.at[lay], sec, strip).wait_recv()

        band = 128
        for part in range(2):
            row = gall[lay, part:part + 1, :]
            base = pltpu.roll(
                jnp.broadcast_to(row, (band, length)), 0, axis=1, stride=1, stride_axis=0
            ).astype(BF16)
            for b in range(length // band):
                at = band * b
                if b:
                    gmat[lay, part, at:at + band, 0:at] = base[:, length - at:]
                gmat[lay, part, at:at + band, at:] = base[:, :length - at]

    def screen_of(lay):
        if lay % 2 == 0:
            src, dst = rows_of[lay // 2]

            @pl.when(sec != lay)
            def _():
                remote(src.at[0], dst, ssend, srecv.at[lay], sec, strip).wait_recv()
            return sincos(dst[...].astype(F32))

        dst = cols_of[lay // 2][1]

        @pl.when(sec != lay)
        def _():
            remote(dst, dst, ssend, srecv.at[lay], sec, strip).wait_recv()

        @pl.when(sec == lay)
        def _():
            most = dst.at[pl.ds(0, strips - 1)]
            remote(most, most, ssend, srecv.at[lay], sec, strip).wait_recv()

        return sincos(jnp.concatenate([dst[s].astype(F32) for s in range(strips)], axis=1))

    def put(fc, value):
        rounded = value.astype(BF16)
        slab[fc * lines:(fc + 1) * lines, :] = rounded
        other = fc ^ 1
        swapped[other * lines:(other + 1) * lines, :] = rounded if fc % 2 == 0 else -rounded

    def screened(lay, load):
        sine, cosine = screen_of(lay)
        for f in range(2):
            re = load(2 * f)
            im = load(2 * f + 1)
            put(2 * f, re * cosine - im * sine)
            put(2 * f + 1, re * sine + im * cosine)

    block = 256

    def across(lay, step):
        per = block // lines

        def body(i, _):
            b = lax.rem(me // per + 1 + i, length // block)
            at = pl.ds(pl.multiple_of(b * block, block), block)
            dims = (((1,), (1,)), ((), ()))
            total = lax.dot_general(
                gmat[lay, 0, at, :], slab[...], dims, preferred_element_type=F32
            ) + lax.dot_general(
                gmat[lay, 1, at, :], swapped[...], dims, preferred_element_type=F32
            )
            sendbuf[step, pl.ds(b * per, per)] = total.reshape(per, lines, wide).astype(BF16)

            def one(j, _):
                peer = b * per + lax.rem(me + j, per)

                @pl.when(peer != me)
                def _():
                    remote(
                        sendbuf.at[step, peer], recvbuf.at[step, me], xsend.at[step],
                        xrecv.at[step], lax.rem(peer, layers), peer // layers,
                    ).start()
                return 0

            lax.fori_loop(0, per, one, 0)
            return 0

        lax.fori_loop(0, length // block, body, 0)

        recvbuf[step, me] = sendbuf[step, me]

    def arrived(step):
        most = recvbuf.at[step, pl.ds(0, count - 1)]
        remote(most, most, xsend.at[step], xrecv.at[step], sec, strip).wait_recv()
        if wide == 128:
            lane = lax.broadcasted_iota(jnp.int32, (lines, wide), 1) // lines
            for g in range(count // 4):
                pieces = [recvbuf[step, 4 * g + q].astype(F32) for q in range(4)]
                for fc in range(4):
                    out = None
                    for q in range(4):
                        shift = ((q - fc) * lines) % wide
                        moved = pltpu.roll(pieces[q], shift, axis=1) if shift else pieces[q]
                        out = moved if out is None else jnp.where(lane == q, moved, out)
                    rounded = out.astype(BF16)
                    at = slice(g * wide, (g + 1) * wide)
                    slab[fc * lines:(fc + 1) * lines, at] = rounded
                    other = fc ^ 1
                    swapped[other * lines:(other + 1) * lines, at] = (
                        rounded if fc % 2 == 0 else -rounded
                    )
        else:
            for fc in range(4):
                put(fc, jnp.concatenate(
                    [
                        recvbuf[step, d].astype(F32)[:, fc * lines:(fc + 1) * lines]
                        for d in range(count)
                    ],
                    axis=1,
                ))

    def along(lay):
        def body(b, _):
            at = pl.ds(pl.multiple_of(b * block, block), block)
            mid[:, at] = jnp.dot(
                slab[...], gmat[lay, 0, :, at], preferred_element_type=F32
            ) + jnp.dot(swapped[...], gmat[lay, 1, :, at], preferred_element_type=F32)
            return 0

        lax.fori_loop(0, length // block, body, 0)

    build(0)
    screened(0, lambda fc: launch_ref[fc, sec].astype(F32))
    across(0, 0)
    for lay in range(1, layers):
        build(lay)
    for lay in range(1, layers):
        arrived(lay - 1)
        along(lay - 1)
        screened(lay, lambda fc: mid[fc * lines:(fc + 1) * lines, :])
        across(lay, lay)
    arrived(layers - 1)
    along(layers - 1)
    for fc in range(4):
        out_ref[sec, fc] = mid[fc * lines:(fc + 1) * lines, :].astype(BF16)
    for k in range(1, layers):
        a = lax.rem(sec + k, layers)
        remote(out_ref.at[sec], out_ref.at[sec], osend, orecv, a, strip).start()
    most = out_ref.at[pl.ds(0, layers - 1)]
    remote(most, most, osend, orecv, sec, strip).wait()
    for k in range(1, layers):
        remote(g_ref, gall.at[sec], gsend, grecv.at[sec], sec, strip).wait_send()
    for lay in range(layers):
        @pl.when(sec == lay)
        def _(lay=lay):
            if lay % 2 == 0:
                some = rows_of[lay // 2][0].at[pl.ds(0, layers - 1)]
            else:
                some = cols_of[lay // 2][0].at[pl.ds(0, count - 1)]
            remote(some, some, ssend, srecv.at[lay], sec, strip).wait_send()
    for step in range(layers):
        most = sendbuf.at[step, pl.ds(0, count - 1)]
        remote(most, most, xsend.at[step], xrecv.at[step], sec, strip).wait_send()


def propagate(launch, screens, line, layers, strips):
    rows, length = launch.shape[2:]
    lines = rows // layers
    count = layers * strips
    vmem = pl.BlockSpec(memory_space=pltpu.VMEM)
    dma = pltpu.SemaphoreType.DMA
    screen = screens[0]
    return pl.pallas_call(
        functools.partial(propagate_kernel, layers, strips),
        out_shape=jax.ShapeDtypeStruct((layers, 4, lines, length), BF16),
        in_specs=[vmem] * 4,
        out_specs=vmem,
        scratch_shapes=[
            pltpu.VMEM((layers, 8, length), F32),
            pltpu.VMEM((layers, 2, length, length), BF16),
            pltpu.VMEM((lines, length), BF16),
            pltpu.VMEM((strips, lines, rows), BF16),
            pltpu.VMEM((layers, lines, length), BF16),
            pltpu.VMEM((count, lines, rows), BF16),
            pltpu.VMEM((layers // 2 - 1, lines, length), F32),
            pltpu.VMEM((layers // 2 - 1, strips, lines, rows), F32),
            pltpu.VMEM((layers, count, lines, 4 * lines), BF16),
            pltpu.VMEM((layers, count, lines, 4 * lines), BF16),
            pltpu.VMEM((4 * lines, length), BF16),
            pltpu.VMEM((4 * lines, length), BF16),
            pltpu.VMEM((4 * lines, length), F32),
            dma, dma((layers,)), dma, dma((layers,)), dma((layers,)), dma((layers,)), dma, dma,
        ],
        compiler_params=pltpu.CompilerParams(
            collective_id=0, has_side_effects=True, vmem_limit_bytes=56 << 20
        ),
        name="propagate",
    )(
        launch.reshape(4, layers, lines, length),
        screen.reshape(layers, lines, length),
        screen.T.reshape(count, lines, rows),
        line,
    )


def gather_kernel(side, picks_ref, pupil_ref, out_ref):
    for o in range(out_ref.shape[0]):
        pick = picks_ref[o]
        top = pl.multiple_of(pick // side * SUB, SUB)
        left = pick % side * SUB
        tile = pl.multiple_of(left // 128 * 128, 128)
        shift = (128 - left % 128) % 128
        for part in range(4):
            rows = pupil_ref[part, pl.ds(top, SUB), pl.ds(tile, 128)].astype(F32)
            out_ref[o, part] = pltpu.roll(rows, shift, axis=1)[:, :SUB].astype(BF16)


def gather_blocks(pupil, picks):
    vmem = pl.BlockSpec(memory_space=pltpu.VMEM)
    return pl.pallas_call(
        functools.partial(gather_kernel, pupil.shape[-1] // SUB),
        out_shape=jax.ShapeDtypeStruct((picks.shape[0], 4, SUB, SUB), BF16),
        in_specs=[pl.BlockSpec(memory_space=pltpu.SMEM), vmem],
        out_specs=vmem,
        name="gather",
    )(picks, pupil)


def swap_kernel(strips, in_ref, out_ref, send, recv):
    sec = lax.axis_index("layer")
    strip = lax.axis_index("strip")
    barrier = pltpu.get_barrier_semaphore()
    for k in range(1, strips):
        pl.semaphore_signal(
            barrier, inc=1, device_id=(sec, lax.rem(strip + k, strips)), device_id_type=MESH
        )
    pl.semaphore_wait(barrier, strips - 1)
    for k in range(1, strips):
        peer = lax.rem(strip + k, strips)
        pltpu.make_async_remote_copy(
            src_ref=in_ref.at[peer], dst_ref=out_ref.at[strip], send_sem=send, recv_sem=recv,
            device_id=(sec, peer), device_id_type=MESH,
        ).start()
    out_ref[strip] = in_ref[strip]
    most = out_ref.at[pl.ds(0, strips - 1)]
    pltpu.make_async_remote_copy(
        src_ref=most, dst_ref=most, send_sem=send, recv_sem=recv,
        device_id=(sec, strip), device_id_type=MESH,
    ).wait()


def swap_strips(result, strips):
    fields, channels = result.shape[1:]
    vmem = pl.BlockSpec(memory_space=pltpu.VMEM)
    dma = pltpu.SemaphoreType.DMA
    out = pl.pallas_call(
        functools.partial(swap_kernel, strips),
        out_shape=jax.ShapeDtypeStruct((strips, 8, 128), F32),
        in_specs=[vmem],
        out_specs=vmem,
        scratch_shapes=[dma, dma],
        compiler_params=pltpu.CompilerParams(collective_id=1, has_side_effects=True),
        name="swap",
    )(jnp.pad(result, ((0, 0), (0, 8 - fields), (0, 128 - channels))))
    return out[:, :fields, :channels]


def per_device(launch, screens, distance, templates, send_table, send_counts):
    layers = lax.axis_size("layer")
    strips = lax.axis_size("strip")
    sec = lax.axis_index("layer")
    fields = launch.shape[0]
    rows, length = launch.shape[2:]
    line = kernel_line(distance[0], length)
    done = propagate(launch, screens, line, layers, strips)
    pupil = done.transpose(1, 0, 2, 3).reshape(fields, 2, rows, length)
    side = length // SUB
    blocks = gather_blocks(pupil.reshape(2 * fields, rows, length), send_table.reshape(strips))
    flat = blocks.reshape(strips * fields, 2 * SUB * SUB)
    table = jnp.asarray(spot_table(SUB))
    pixels = templates.shape[0]
    spot = jnp.dot(flat, table, preferred_element_type=F32)
    intensity = (spot[:, :pixels] ** 2 + spot[:, pixels:] ** 2).astype(BF16)
    result = jnp.dot(intensity, templates, preferred_element_type=F32)
    result = result.reshape(strips, fields, templates.shape[1])
    live = sec < send_counts[0]
    result = jnp.where(live[:, None, None], result, 0.0)
    received = swap_strips(result, strips)
    return (pupil, received[None, :, None])


def solution(mesh):
    placed = (
        P(None, None, "strip", None),
        P("layer", "strip", None),
        P("layer"),
        P(),
        P("strip", None, "layer"),
        P("strip", None),
    )
    return jax.shard_map(
        per_device,
        mesh=mesh,
        in_specs=placed,
        out_specs=(P(None, None, "strip", None), P("strip", None, "layer", None, None)),
        check_vma=False,
    )
```
